256 devices in a mesh: layer: 4 (over y), row: 8 (over x, core), col: 8 (over z).
Axes of the slice: x: 4, y: 4, z: 8, core: 2. Of those that a mesh axis runs over, the one named last changes fastest.
Arguments:
- l_blocks: bfloat16 [4, 64, 256, 256], P('layer', ('row', 'col')), may hold values from -3 to 3
- l_ids: int32 [4, 64], P('layer'), may hold values from 0 to 127, as said below
- u_blocks: bfloat16 [4, 64, 256, 256], P('layer', ('row', 'col')), may hold values from -3 to 3
- u_ids: int32 [4, 64], P('layer'), may hold values from 0 to 127, as said below
- inv_upper: bfloat16 [8, 256, 256], replicated, as said below
- inv_lower: bfloat16 [8, 256, 256], replicated, as said below
- row_order: int32 [16], replicated, may hold values from 0 to 15, as said below
- col_order: int32 [16], replicated, may hold values from 0 to 15, as said below
- front_in: float32 [16, 16, 256, 256], P('row', 'col', 'layer'), may hold values from -6 to 6
- leaf_lower: bfloat16 [256, 1024, 1024], P(('layer', 'row', 'col')), may hold values from -6 to 6
- leaf_upper: bfloat16 [256, 1024, 1024], P(('layer', 'row', 'col')), may hold values from -0.1875 to 0.1875
- leaf_front: bfloat16 [256, 1024, 1024], P(('layer', 'row', 'col')), may hold values from -6 to 6
Outputs:
- front_out: float32 [16, 16, 256, 256], P('row', 'col', 'layer')
- leaf_out: bfloat16 [256, 1024, 1024], P(('layer', 'row', 'col'))
The draws below stay inside these ranges and needn't reach their ends.
Inputs may be any that keep to these rules, and one draw needn't show every extreme that they name: `l_ids`: within a layer the ids are distinct; the entry at index r * 8 + c has i = row_order[r * 2 + p] for some p < 2. `u_ids`: within a layer the ids are distinct; the entry at index r * 8 + c has j = col_order[c * 2 + q] for some q < 2. `row_order`: A permutation of the tile rows. `col_order`: A permutation of the tile columns. `inv_upper`: each block is upper triangular with a positive diagonal. `inv_lower`: each block is lower triangular with a positive diagonal.
All inputs are finite; a program needn't handle non-finite values.
Results may differ from the reference program's by a relative error of at most 0.0095.
Values may be sent and summed in bfloat16 or wider, within the bound.
No kernel may reach another device: no remote copies, remote signals or barrier semaphores. Data moves between devices by JAX's collectives and lax.ppermute only.
A program may use at most 128 MiB of HBM per device.

```python
import jax
import jax.numpy as jnp
from jax import lax

TB = 256
LF = 1024
KL = 1024
NT = 16
KB = 8
RPG = 2
CPG = 2
NBL = 64
LEAVES = 256
N_LAYER = 4
N_ROW = 8
N_COL = 8


def order_perm(key, salt):
    return jax.random.permutation(jax.random.fold_in(key, salt), NT).astype(jnp.int32)


def draw_row_order(key, part):
    return order_perm(key, 101)


def draw_col_order(key, part):
    return order_perm(key, 202)


def draw_l_ids(key, part):
    owned = order_perm(key, 101).reshape(N_ROW, RPG)
    keys = jax.random.split(jax.random.fold_in(key, 303), N_LAYER * N_ROW)
    picks = jax.vmap(lambda one: jax.random.permutation(one, RPG * KB)[:N_COL])(keys)
    picks = picks.reshape(N_LAYER, N_ROW, N_COL).astype(jnp.int32)
    grid_rows = jnp.arange(N_ROW, dtype=jnp.int32)[None, :, None]
    tile_row = owned[grid_rows, picks // KB]
    return (tile_row * KB + picks % KB).reshape(N_LAYER, N_ROW * N_COL).astype(jnp.int32)


def draw_u_ids(key, part):
    owned = order_perm(key, 202).reshape(N_COL, CPG)
    keys = jax.random.split(jax.random.fold_in(key, 404), N_LAYER * N_COL)
    picks = jax.vmap(lambda one: jax.random.permutation(one, CPG * KB)[:N_ROW])(keys)
    picks = picks.reshape(N_LAYER, N_COL, N_ROW).astype(jnp.int32)
    grid_cols = jnp.arange(N_COL, dtype=jnp.int32)[None, :, None]
    tile_col = owned[grid_cols, picks // KB]
    ids = picks % KB * NT + tile_col
    return ids.transpose(0, 2, 1).reshape(N_LAYER, N_ROW * N_COL).astype(jnp.int32)


def triangle(key, salt, upper_part):
    key_diag, key_off = jax.random.split(jax.random.fold_in(key, salt))
    diag = jax.random.uniform(key_diag, (KB, TB), minval=0.7, maxval=1.4)
    off = jnp.clip(jax.random.normal(key_off, (KB, TB, TB)), -4.0, 4.0) * (0.5 / TB ** 0.5)
    rows = jnp.arange(TB)[:, None]
    cols = jnp.arange(TB)[None, :]
    if upper_part:
        keep = cols > rows
    else:
        keep = cols < rows
    eye = (rows == cols).astype(jnp.float32)
    full = jnp.where(keep[None], off, 0.0) + diag[:, :, None] * eye[None]
    return full.astype(jnp.bfloat16)


def draw_inv_upper(key, part):
    return triangle(key, 505, True)


def draw_inv_lower(key, part):
    return triangle(key, 606, False)


def block_levels(rng, extent, shards, low, high):
    loudness, own = 1.0, jax.random.fold_in(rng, 6)
    for axis_at, shards_of in shards:
        heights = jnp.exp(jax.random.uniform(jax.random.fold_in(own, axis_at), (shards_of,), jnp.float32, low / len(shards), high / len(shards)))
        loudness = loudness * jnp.repeat(heights, extent[axis_at] // shards_of).reshape([-1 if axis == axis_at else 1 for axis in range(len(extent))])
    return loudness


def centred(key, extent, deviation, limit, cuts=(), kind=jnp.bfloat16):
    result = jax.random.normal(key, extent, jnp.float32) * deviation
    if len(cuts) > 0:
        result = block_levels(key, extent, cuts, -0.22, 0.18) * result
    return jnp.clip(result, min=-limit, max=limit).astype(kind)


def setup_inputs(seed: int = 0) -> dict:
    key_of = jax.random.split(jax.random.key(seed), 13)
    l_blocks = centred(key_of[0], (N_LAYER, NBL, TB, TB), 0.2, 3.0, ((0, 4), (1, 64)))
    l_ids = draw_l_ids(jax.random.fold_in(key_of[12], 71), 0)
    u_blocks = centred(key_of[2], (N_LAYER, NBL, TB, TB), 0.2, 3.0, ((0, 4), (1, 64)))
    u_ids = draw_u_ids(jax.random.fold_in(key_of[12], 71), 0)
    inv_upper = draw_inv_upper(jax.random.fold_in(key_of[12], 71), 0)
    inv_lower = draw_inv_lower(jax.random.fold_in(key_of[12], 71), 0)
    row_order = draw_row_order(jax.random.fold_in(key_of[12], 71), 0)
    col_order = draw_col_order(jax.random.fold_in(key_of[12], 71), 0)
    front_in = centred(key_of[8], (NT, NT, TB, TB), 1.0, 6.0, ((0, 8), (1, 8), (2, 4)), jnp.float32)
    leaf_lower = centred(key_of[9], (LEAVES, LF, KL), 1.0, 6.0, ((0, 256),))
    leaf_upper = centred(key_of[10], (LEAVES, KL, LF), KL ** -0.5, 0.1875, ((0, 256),))
    leaf_front = centred(key_of[11], (LEAVES, LF, LF), 1.0, 6.0, ((0, 256),))
    return {"l_blocks": l_blocks, "l_ids": l_ids, "u_blocks": u_blocks, "u_ids": u_ids, "inv_upper": inv_upper, "inv_lower": inv_lower, "row_order": row_order, "col_order": col_order, "front_in": front_in, "leaf_lower": leaf_lower, "leaf_upper": leaf_upper, "leaf_front": leaf_front}


def reference(l_blocks, l_ids, u_blocks, u_ids, inv_upper, inv_lower, row_order, col_order, front_in, leaf_lower, leaf_upper, leaf_front):
    highest = lax.Precision.HIGHEST
    schur = jnp.zeros((NT * TB, NT * TB), jnp.float32)
    for layer in range(N_LAYER):
        ids_low = l_ids[layer].astype(jnp.int32)
        ids_up = u_ids[layer].astype(jnp.int32)
        inv_u = inv_upper[ids_low % KB].astype(jnp.float32)
        lower = jnp.einsum("mab,mbc->mac", l_blocks[layer].astype(jnp.float32), inv_u, precision=highest).astype(jnp.bfloat16)
        inv_l = inv_lower[ids_up // NT].astype(jnp.float32)
        upper = jnp.einsum("mab,mbc->mac", inv_l, u_blocks[layer].astype(jnp.float32), precision=highest).astype(jnp.bfloat16)
        lpanel = jnp.zeros((NT * KB, TB, TB), jnp.bfloat16).at[ids_low].set(lower)
        lpanel = lpanel.reshape(NT, KB, TB, TB).transpose(0, 2, 1, 3).reshape(NT * TB, KB * TB)
        upanel = jnp.zeros((KB * NT, TB, TB), jnp.bfloat16).at[ids_up].set(upper)
        upanel = upanel.reshape(KB, NT, TB, TB).transpose(0, 2, 1, 3).reshape(KB * TB, NT * TB)
        schur = schur + jnp.dot(lpanel.astype(jnp.float32), upanel.astype(jnp.float32), precision=highest)
    tiles = schur.reshape(NT, TB, NT, TB).transpose(0, 2, 1, 3)
    tiles = tiles[row_order.astype(jnp.int32)][:, col_order.astype(jnp.int32)]
    front_out = front_in - tiles
    update = jnp.einsum("nab,nbc->nac", leaf_lower.astype(jnp.float32), leaf_upper.astype(jnp.float32), precision=highest)
    leaf_out = (leaf_front.astype(jnp.float32) - update).astype(jnp.bfloat16)
    return front_out, leaf_out
```

```python
import functools

import jax
import jax.numpy as jnp
from jax import lax
from jax.experimental import pallas as pl
from jax.experimental.pallas import tpu as pltpu
from jax.sharding import PartitionSpec as P


VMEM_LIMIT = 16 << 20
VMEM = pl.BlockSpec(memory_space=pltpu.VMEM)
SMEM = pl.BlockSpec(memory_space=pltpu.SMEM)


def hop(x, axis, size, d):
    return lax.ppermute(x, axis, [(i, (i + d) % size) for i in range(size)])


def pal(body, outs, ins, args, flops=0, moved=0):
    return pl.pallas_call(
        body,
        out_shape=outs,
        in_specs=ins,
        out_specs=jax.tree.map(lambda _: VMEM, outs),
        cost_estimate=pl.CostEstimate(flops=flops, bytes_accessed=moved, transcendentals=0),
        compiler_params=pltpu.CompilerParams(vmem_limit_bytes=VMEM_LIMIT),
    )(*args)


def upper_body(ids, order, inv, own, far, swapped, out, *, tiles_side, rows, cols):
    r = lax.axis_index("row")
    c = lax.axis_index("col")
    tile = own.shape[-1]
    out[...] = jnp.zeros_like(out)
    second = order[2 * c + 1]
    half = rows // 2
    for n in range(rows):
        if n == 0:
            block, src = own[...], r
        elif n < half:
            block, src = far[n - 1], lax.rem(r + rows - 2 * n, rows)
        else:
            block, src = swapped[n - half], lax.rem(lax.rem(r + 1, 2) + (r - lax.rem(r, 2)) + rows - 2 * (n - half), rows)
        ident = ids[0, src * cols + c]
        k = lax.div(ident, tiles_side)
        q = jnp.where(lax.rem(ident, tiles_side) == second, 1, 0)
        prod = jnp.dot(inv[k], block, preferred_element_type=jnp.float32).astype(jnp.bfloat16)
        out[k, :, pl.ds(pl.multiple_of(q * tile, tile), tile)] = prod


def add_lower(block, d, ids, order, inv, up, acc, panels, cols):
    r = lax.axis_index("row")
    c = lax.axis_index("col")
    ident = ids[0, r * cols + lax.rem(c + cols - d, cols)]
    k = lax.rem(ident, panels)
    p = jnp.where(lax.div(ident, panels) == order[2 * r + 1], 1, 0)
    low = jnp.dot(block, inv[k], preferred_element_type=jnp.float32).astype(jnp.bfloat16)
    acc[p] += jnp.dot(low, up[k], preferred_element_type=jnp.float32)


def near_body(ids, order, inv, up, b0, b1, b2, b3, b4, acc, *, dist, panels, cols):
    acc[...] = jnp.zeros_like(acc)
    for b, d in zip((b0, b1, b2, b3, b4), dist):
        add_lower(b[...], d, ids, order, inv, up, acc, panels, cols)


def far_body(ids, order, inv, up, b0, b1, ha, hb, acc_in, s1, s2, s3, own, acc, *, panels, cols, layers):
    acc[...] = acc_in[...]
    add_lower(b0[...], 3, ids, order, inv, up, acc, panels, cols)
    add_lower(b1[...], -3, ids, order, inv, up, acc, panels, cols)
    add_lower(jnp.concatenate([ha[...], hb[...]], axis=0), 4, ids, order, inv, up, acc, panels, cols)
    layer = lax.axis_index("layer")
    part = own.shape[2]
    tile = own.shape[3]
    for d, dst in ((2, s2), (1, s1), (3, s3), (0, own)):
        at = pl.multiple_of(lax.rem(layer + d, layers) * part, part)
        for p in range(2):
            for q in range(2):
                dst[p, q] = acc[p, pl.ds(at, part), q * tile : (q + 1) * tile].astype(dst.dtype)


def shards(
    l_blocks,
    l_ids,
    u_blocks,
    u_ids,
    inv_upper,
    inv_lower,
    row_order,
    col_order,
    front_in,
    leaf_lower,
    leaf_upper,
    leaf_front,
):
    tile = l_blocks.shape[-1]
    panels = inv_upper.shape[0]
    tiles_side = row_order.shape[0]
    part = front_in.shape[2]
    rows = lax.axis_size("row")
    cols = lax.axis_size("col")
    layers = lax.axis_size("layer")
    bf, f32 = jnp.bfloat16, jnp.float32
    sds = jax.ShapeDtypeStruct

    z = functools.partial(hop, axis="col", size=cols)
    b = l_blocks[0, 0]
    m2, p2 = z(b, d=2), z(b, d=-2)
    m1, p1 = z(b, d=1), z(b, d=-1)
    m3, p3 = z(m2, d=1), z(p2, d=-1)
    ha, hb = z(m2[: tile // 2], d=2), z(p2[tile // 2 :], d=-2)

    x = functools.partial(hop, axis="row", size=rows)
    u = u_blocks[0, 0]
    far = [x(u, d=2 * n) for n in range(1, rows // 2)]
    stack = jnp.stack([u, *far])
    swapped = lax.ppermute(stack, "row", [(i, i ^ 1) for i in range(rows)])

    up = pal(
        functools.partial(upper_body, tiles_side=tiles_side, rows=rows, cols=cols),
        sds((panels, tile, 2 * tile), bf),
        [SMEM, SMEM, VMEM, VMEM, VMEM, VMEM],
        (u_ids, col_order, inv_lower, u, stack[1:], swapped),
        flops=2 * 8 * tile**3,
        moved=4 << 20,
    )
    acc = pal(
        functools.partial(near_body, dist=(0, 1, -1, 2, -2), panels=panels, cols=cols),
        sds((2, tile, 2 * tile), f32),
        [SMEM, SMEM] + [VMEM] * 7,
        (l_ids, row_order, inv_upper, up, b, m1, p1, m2, p2),
        flops=2 * 5 * 3 * tile**3,
        moved=4 << 20,
    )
    piece = (2, 2, part, tile)
    s1, s2, s3, own = pl.pallas_call(
        functools.partial(far_body, panels=panels, cols=cols, layers=layers),
        out_shape=(sds(piece, bf), sds(piece, bf), sds(piece, bf), sds(piece, f32)),
        in_specs=[SMEM, SMEM] + [VMEM] * 7,
        out_specs=(VMEM,) * 4,
        scratch_shapes=[pltpu.VMEM((2, tile, 2 * tile), f32)],
        cost_estimate=pl.CostEstimate(flops=2 * 3 * 3 * tile**3, bytes_accessed=4 << 20, transcendentals=0),
        compiler_params=pltpu.CompilerParams(vmem_limit_bytes=VMEM_LIMIT),
    )(l_ids, row_order, inv_upper, up, m3, p3, ha, hb, acc)
    y = functools.partial(hop, axis="layer", size=layers)
    r2, r1, r3 = y(s2, d=2), y(s1, d=1), y(s3, d=3)
    front_out = front_in - (own + r1.astype(f32) + r2.astype(f32) + r3.astype(f32))

    update = jnp.dot(leaf_lower[0], leaf_upper[0], preferred_element_type=f32)
    leaf_out = (leaf_front[0].astype(f32) - update).astype(bf)[None]
    return (front_out, leaf_out)


def solution(mesh):
    return jax.shard_map(
        shards,
        mesh=mesh,
        in_specs=(
            P("layer", ("row", "col"), None, None),
            P("layer", None),
            P("layer", ("row", "col"), None, None),
            P("layer", None),
            P(),
            P(),
            P(),
            P(),
            P("row", "col", "layer", None),
            P(("layer", "row", "col"), None, None),
            P(("layer", "row", "col"), None, None),
            P(("layer", "row", "col"), None, None),
        ),
        out_specs=(P("row", "col", "layer", None), P(("layer", "row", "col"), None, None)),
        check_vma=False,
    )
```

```python
import functools

import jax
import jax.numpy as jnp
from jax import lax
from jax.experimental import pallas as pl
from jax.experimental.pallas import tpu as pltpu
from jax.sharding import PartitionSpec as P


U_FLIPS = (0, 2, 6, 4, 1, 3, 7, 5)
L_STEPS = ((0, 0), (0, 1), (0, -1), (4, 0), (4, 1), (4, -1), (0, 2), (0, -2))
COLS = 8
BLOCKS = 64
TILES = 16
VMEM_LIMIT = 16 << 20
VMEM = pl.BlockSpec(memory_space=pltpu.VMEM)
SMEM = pl.BlockSpec(memory_space=pltpu.SMEM)


def swap_with(x, axis, size, partner):
    return lax.ppermute(x, axis, [(i, partner(i) % size) for i in range(size)])


def other_pair(i):
    return i + 1 if i % 2 else i - 1


def call(body, outs, ins, args, flops, moved, scratch=(), out_specs=None):
    return pl.pallas_call(
        body,
        out_shape=outs,
        in_specs=ins,
        out_specs=out_specs or jax.tree.map(lambda _: VMEM, outs),
        scratch_shapes=list(scratch),
        cost_estimate=pl.CostEstimate(flops=flops, bytes_accessed=moved, transcendentals=0),
        compiler_params=pltpu.CompilerParams(vmem_limit_bytes=VMEM_LIMIT),
    )(*args)


def add_upper(block, n, meta, inv, up):
    r = lax.axis_index("row")
    c = lax.axis_index("col")
    tile = inv.shape[-1]
    ident = meta[0, (r ^ U_FLIPS[n]) * COLS + c]
    k = lax.div(ident, TILES)
    q = jnp.where(lax.rem(ident, TILES) == meta[0, 2 * BLOCKS + 2 * c + 1], 1, 0)
    prod = jnp.dot(inv[k], block, preferred_element_type=jnp.float32).astype(jnp.bfloat16)
    up[k, :, pl.ds(pl.multiple_of(q * tile, tile), tile)] = prod


def add_lower(block, n, meta, inv, up, acc):
    r = lax.axis_index("row")
    c = lax.axis_index("col")
    panels = up.shape[0]
    whole, sided = L_STEPS[n]
    step = whole + sided * (1 - 2 * lax.rem(c, 2))
    ident = meta[0, BLOCKS + r * COLS + lax.rem(c + step + COLS, COLS)]
    k = lax.rem(ident, panels)
    p = jnp.where(lax.div(ident, panels) == meta[0, 2 * BLOCKS + TILES + 2 * r + 1], 1, 0)
    low = jnp.dot(block, inv[panels + k], preferred_element_type=jnp.float32).astype(jnp.bfloat16)
    acc[p] += jnp.dot(low, up[k], preferred_element_type=jnp.float32)


def near_body(meta, inv, *refs):
    uppers, lowers, (up, acc) = refs[: len(U_FLIPS)], refs[len(U_FLIPS) : -2], refs[-2:]
    up[...] = jnp.zeros_like(up)
    acc[...] = jnp.zeros_like(acc)
    for n, ref in enumerate(uppers):
        add_upper(ref[...], n, meta, inv, up)
    for n, ref in enumerate(lowers):
        add_lower(ref[...], n, meta, inv, up, acc)


def mid_body(meta, inv, up, acc_in, *refs, first):
    acc = refs[-1]
    acc[...] = acc_in[...]
    for n, ref in enumerate(refs[:-1]):
        add_lower(ref[...], first + n, meta, inv, up, acc)


def far_body(meta, inv, up, acc_in, *refs, first):
    lowers, (s1, s2, s3, own, acc) = refs[:-5], refs[-5:]
    acc[...] = acc_in[...]
    for n, ref in enumerate(lowers):
        add_lower(ref[...], first + n, meta, inv, up, acc)
    layer = lax.axis_index("layer")
    part, tile = own.shape[2:]
    for flip, dst in ((2, s2), (1, s1), (3, s3), (0, own)):
        at = pl.multiple_of((layer ^ flip) * part, part)
        for p in range(2):
            for q in range(2):
                dst[p, q] = acc[p, pl.ds(at, part), q * tile : (q + 1) * tile].astype(dst.dtype)


def program(
    l_blocks,
    l_ids,
    u_blocks,
    u_ids,
    inv_upper,
    inv_lower,
    row_order,
    col_order,
    front_in,
    leaf_lower,
    leaf_upper,
    leaf_front,
):
    tile = l_blocks.shape[-1]
    panels = inv_upper.shape[0]
    part = front_in.shape[2]
    rows = lax.axis_size("row")
    cols = lax.axis_size("col")
    layers = lax.axis_size("layer")
    bf, f32 = jnp.bfloat16, jnp.float32
    sds = jax.ShapeDtypeStruct

    b = l_blocks[0, 0]
    u = u_blocks[0, 0]
    b4 = swap_with(b, "col", cols, lambda i: i + cols // 2)
    be = swap_with(b, "col", cols, lambda i: i ^ 1)
    bo = swap_with(b, "col", cols, other_pair)
    ue = swap_with(u, "row", rows, lambda i: i ^ 2)
    uo = swap_with(u, "row", rows, lambda i: i ^ 6)
    u2 = swap_with(u, "row", rows, lambda i: i ^ 4)
    ours = (u, ue, uo, u2)
    fe = swap_with(bo, "col", cols, lambda i: i ^ 1)
    fo = swap_with(be, "col", cols, other_pair)
    ge = swap_with(b4, "col", cols, lambda i: i ^ 1)
    go = swap_with(b4, "col", cols, other_pair)
    near, mid, far = (b, be, bo, b4), (), (ge, go, fe, fo)
    theirs = tuple(swap_with(x, "row", rows, lambda i: i ^ 1) for x in ours)
    meta = jnp.concatenate([u_ids, l_ids, col_order[None], row_order[None]], axis=1)
    invs = jnp.concatenate([inv_lower, inv_upper])

    up, acc = call(
        near_body,
        (sds((panels, tile, 2 * tile), bf), sds((2, tile, 2 * tile), f32)),
        [SMEM] + [VMEM] * (1 + 8 + len(near)),
        (meta, invs, *ours, *theirs, *near),
        flops=2 * (8 + 3 * len(near)) * tile**3,
        moved=4 << 20,
    )
    if mid:
        acc = call(
            functools.partial(mid_body, first=len(near)),
            sds((2, tile, 2 * tile), f32),
            [SMEM] + [VMEM] * (3 + len(mid)),
            (meta, invs, up, acc, *mid),
            flops=2 * 3 * len(mid) * tile**3,
            moved=4 << 20,
        )
    piece = (2, 2, part, tile)
    s1, s2, s3, own = call(
        functools.partial(far_body, first=len(near) + len(mid)),
        (sds(piece, bf), sds(piece, bf), sds(piece, bf), sds(piece, f32)),
        [SMEM] + [VMEM] * (3 + len(far)),
        (meta, invs, up, acc, *far),
        flops=2 * 3 * len(far) * tile**3,
        moved=4 << 20,
        scratch=[pltpu.VMEM((2, tile, 2 * tile), f32)],
    )
    r2 = swap_with(s2, "layer", layers, lambda i: i ^ 2)
    r1 = swap_with(s1, "layer", layers, lambda i: i ^ 1)
    r3 = swap_with(s3, "layer", layers, lambda i: i ^ 3)
    front_out = front_in - (own + r1.astype(f32) + r2.astype(f32) + r3.astype(f32))

    update = jnp.dot(leaf_lower[0], leaf_upper[0], preferred_element_type=f32)
    leaf_out = (leaf_front[0].astype(f32) - update).astype(bf)[None]
    return (front_out, leaf_out)


def solution(mesh):
    return jax.shard_map(
        program,
        mesh=mesh,
        in_specs=(
            P("layer", ("row", "col"), None, None),
            P("layer", None),
            P("layer", ("row", "col"), None, None),
            P("layer", None),
            P(),
            P(),
            P(),
            P(),
            P("row", "col", "layer", None),
            P(("layer", "row", "col"), None, None),
            P(("layer", "row", "col"), None, None),
            P(("layer", "row", "col"), None, None),
        ),
        out_specs=(P("row", "col", "layer", None), P(("layer", "row", "col"), None, None)),
        check_vma=False,
    )
```

```python
import functools

import jax
import jax.numpy as jnp
from jax import lax
from jax.experimental import pallas as pl
from jax.experimental.pallas import tpu as pltpu
from jax.sharding import PartitionSpec as P


U_FLIPS = (0, 2, 6, 4, 1, 3, 7, 5)
L_STEPS = ((0, 0), (0, 1), (0, -1), (4, 0), (4, 1), (4, -1), (0, 2), (0, -2))
COLS = 8
BLOCKS = 64
TILES = 16
VMEM_LIMIT = 16 << 20
VMEM = pl.BlockSpec(memory_space=pltpu.VMEM)
SMEM = pl.BlockSpec(memory_space=pltpu.SMEM)


def swap_with(x, axis, size, partner):
    return lax.ppermute(x, axis, [(i, partner(i) % size) for i in range(size)])


def other_pair(i):
    return i + 1 if i % 2 else i - 1


def call(body, outs, ins, args, flops, moved, scratch=(), aliases=None):
    return pl.pallas_call(
        body,
        out_shape=outs,
        in_specs=ins,
        out_specs=jax.tree.map(lambda _: VMEM, outs),
        input_output_aliases=aliases or {},
        scratch_shapes=list(scratch),
        cost_estimate=pl.CostEstimate(flops=flops, bytes_accessed=moved, transcendentals=0),
        compiler_params=pltpu.CompilerParams(vmem_limit_bytes=VMEM_LIMIT),
    )(*args)


def add_upper(block, n, meta, inv, up):
    r = lax.axis_index("row")
    c = lax.axis_index("col")
    tile = inv.shape[-1]
    ident = meta[0, (r ^ U_FLIPS[n]) * COLS + c]
    k = lax.div(ident, TILES)
    q = jnp.where(lax.rem(ident, TILES) == meta[0, 2 * BLOCKS + 2 * c + 1], 1, 0)
    prod = jnp.dot(inv[k], block, preferred_element_type=jnp.float32).astype(jnp.bfloat16)
    up[k, :, pl.ds(pl.multiple_of(q * tile, tile), tile)] = prod


def add_lower(block, n, meta, inv, up, acc):
    r = lax.axis_index("row")
    c = lax.axis_index("col")
    panels = up.shape[0]
    whole, sided = L_STEPS[n]
    step = whole + sided * (1 - 2 * lax.rem(c, 2))
    ident = meta[0, BLOCKS + r * COLS + lax.rem(c + step + COLS, COLS)]
    k = lax.rem(ident, panels)
    p = jnp.where(lax.div(ident, panels) == meta[0, 2 * BLOCKS + TILES + 2 * r + 1], 1, 0)
    low = jnp.dot(block, inv[panels + k], preferred_element_type=jnp.float32).astype(jnp.bfloat16)
    acc[p] += jnp.dot(low, up[k], preferred_element_type=jnp.float32)


def early_body(meta, inv, *refs):
    up = refs[-1]
    up[...] = jnp.zeros_like(up)
    for n, ref in enumerate(refs[:-1]):
        add_upper(ref[...], n, meta, inv, up)


def near_body(meta, inv, up_in, *refs):
    half = len(U_FLIPS) // 2
    uppers, lowers, (up, acc) = refs[:half], refs[half:-2], refs[-2:]
    acc[...] = jnp.zeros_like(acc)
    for n, ref in enumerate(uppers):
        add_upper(ref[...], half + n, meta, inv, up)
    for n, ref in enumerate(lowers):
        add_lower(ref[...], n, meta, inv, up, acc)


def far_body(meta, inv, up, acc_in, *refs, first):
    lowers, (s1, s2, s3, own, acc) = refs[:-5], refs[-5:]
    acc[...] = acc_in[...]
    for n, ref in enumerate(lowers):
        add_lower(ref[...], first + n, meta, inv, up, acc)
    layer = lax.axis_index("layer")
    part, tile = own.shape[2:]
    for flip, dst in ((2, s2), (1, s1), (3, s3), (0, own)):
        at = pl.multiple_of((layer ^ flip) * part, part)
        for p in range(2):
            for q in range(2):
                dst[p, q] = acc[p, pl.ds(at, part), q * tile : (q + 1) * tile].astype(dst.dtype)


def program(
    l_blocks,
    l_ids,
    u_blocks,
    u_ids,
    inv_upper,
    inv_lower,
    row_order,
    col_order,
    front_in,
    leaf_lower,
    leaf_upper,
    leaf_front,
):
    tile = l_blocks.shape[-1]
    panels = inv_upper.shape[0]
    part = front_in.shape[2]
    rows = lax.axis_size("row")
    cols = lax.axis_size("col")
    layers = lax.axis_size("layer")
    bf, f32 = jnp.bfloat16, jnp.float32
    sds = jax.ShapeDtypeStruct

    b = l_blocks[0, 0]
    u = u_blocks[0, 0]
    b4 = swap_with(b, "col", cols, lambda i: i + cols // 2)
    be = swap_with(b, "col", cols, lambda i: i ^ 1)
    bo = swap_with(b, "col", cols, other_pair)
    ue = swap_with(u, "row", rows, lambda i: i ^ 2)
    uo = swap_with(u, "row", rows, lambda i: i ^ 6)
    u2 = swap_with(u, "row", rows, lambda i: i ^ 4)
    ours = (u, ue, uo, u2)
    fe = swap_with(bo, "col", cols, lambda i: i ^ 1)
    fo = swap_with(be, "col", cols, other_pair)
    ge = swap_with(b4, "col", cols, lambda i: i ^ 1)
    go = swap_with(b4, "col", cols, other_pair)
    near, far = (b, be, bo, b4), (ge, go, fe, fo)
    theirs = tuple(swap_with(x, "row", rows, lambda i: i ^ 1) for x in ours)
    meta = jnp.concatenate([u_ids, l_ids, col_order[None], row_order[None]], axis=1)
    invs = jnp.concatenate([inv_lower, inv_upper])

    panel = sds((panels, tile, 2 * tile), bf)
    up = call(
        early_body,
        panel,
        [SMEM] + [VMEM] * (1 + len(ours)),
        (meta, invs, *ours),
        flops=2 * 4 * tile**3,
        moved=4 << 20,
    )
    up, acc = call(
        near_body,
        (panel, sds((2, tile, 2 * tile), f32)),
        [SMEM] + [VMEM] * (2 + len(theirs) + len(near)),
        (meta, invs, up, *theirs, *near),
        flops=2 * (4 + 3 * len(near)) * tile**3,
        moved=4 << 20,
        aliases={2: 0},
    )
    piece = (2, 2, part, tile)
    s1, s2, s3, own = call(
        functools.partial(far_body, first=len(near)),
        (sds(piece, bf), sds(piece, bf), sds(piece, bf), sds(piece, f32)),
        [SMEM] + [VMEM] * (3 + len(far)),
        (meta, invs, up, acc, *far),
        flops=2 * 3 * len(far) * tile**3,
        moved=4 << 20,
        scratch=[pltpu.VMEM((2, tile, 2 * tile), f32)],
    )
    r2 = swap_with(s2, "layer", layers, lambda i: i ^ 2)
    r1 = swap_with(s1, "layer", layers, lambda i: i ^ 1)
    r3 = swap_with(s3, "layer", layers, lambda i: i ^ 3)
    front_out = front_in - (own + r1.astype(f32) + r2.astype(f32) + r3.astype(f32))

    update = jnp.dot(leaf_lower[0], leaf_upper[0], preferred_element_type=f32)
    leaf_out = (leaf_front[0].astype(f32) - update).astype(bf)[None]
    return (front_out, leaf_out)


def solution(mesh):
    return jax.shard_map(
        program,
        mesh=mesh,
        in_specs=(
            P("layer", ("row", "col"), None, None),
            P("layer", None),
            P("layer", ("row", "col"), None, None),
            P("layer", None),
            P(),
            P(),
            P(),
            P(),
            P("row", "col", "layer", None),
            P(("layer", "row", "col"), None, None),
            P(("layer", "row", "col"), None, None),
            P(("layer", "row", "col"), None, None),
        ),
        out_specs=(P("row", "col", "layer", None), P(("layer", "row", "col"), None, None)),
        check_vma=False,
    )
```
